256 devices in a mesh: group: 8 (over z), member: 32 (over x, y, core).
Axes of the slice: x: 4, y: 4, z: 8, core: 2. Of those that a mesh axis runs over, the one named last changes fastest.
Arguments:
- diag_tiles: bfloat16 [4096, 4, 128, 128], P(('group', 'member')), may hold values from -0.21875 to 0.21875
- diag_cols: int32 [4096, 4], P(('group', 'member')), may hold values from 0 to 15
- offd_tiles: bfloat16 [4096, 2, 128, 128], P(('group', 'member')), may hold values from -0.21875 to 0.21875
- offd_cols: int32 [4096, 2], P(('group', 'member')), may hold values from 0 to 31, as said below
- offd_count: int32 [4096], P(('group', 'member')), may hold values from 0 to 2
- p_tiles: bfloat16 [4096, 2, 128, 128], P(('group', 'member')), may hold values from -2 to 2
- p_cols: int32 [4096, 2], P(('group', 'member')), may hold values from 0 to 255, as said below
- send_rows: int32 [256, 32, 1], P(('group', 'member')), may hold values from 0 to 15
- coarse_cols: int32 [256, 8], replicated, may hold values from 0 to 255, as said below
Outputs:
- coarse_tiles: float32 [256, 8, 128, 128], P(('group', 'member'))
The draws below stay inside these ranges and needn't reach their ends.
Inputs may be any that keep to these rules, and one draw needn't show every extreme that they name: `p_cols`: the 2 entries of fine block row f on group g and member m are distinct coarse rows h * 32 + m with h one of g, (g + 1) % 8, (g + 4) % 8. `offd_cols`: A remote tile of a fine block row on member m reads a row sent by member (m - 1) % 32, (m + 1) % 32 or (m + 16) % 32. `coarse_cols`: the 8 entries of coarse row h * 32 + m are distinct; they are that row itself and the rows ((h + 1) % 8) * 32 + m, ((h - 1) % 8) * 32 + m, ((h + 4) % 8) * 32 + m, then four rows h2 * 32 + m2 with h2 among h - 1, h, h + 1, h + 4 and m2 among m - 1, m + 1, m + 32 // 2 (both modulo their counts).
All inputs are finite; a program needn't handle non-finite values.
Results may differ from the reference program's by a relative error of at most 0.005.
Values may be sent and summed in bfloat16 or wider, within the bound.
No kernel may reach another device: no remote copies, remote signals or barrier semaphores. Data moves between devices by JAX's collectives and lax.ppermute only.
A program may use at most 128 MiB of HBM per device.

```python
import jax
import jax.numpy as jnp
from jax import lax

TILE = 128
ROWS = 16
DIAG = 4
OFFD = 2
PTILES = 2
CTILES = 8
SEND = 1
MEMBERS = 32
FINE = 4096
COARSE = 256
N_GROUP = 8
N_MEMBER = 32


def draw_offd_cols(key, part):
    fine = ROWS * N_GROUP * N_MEMBER
    member_idx = jnp.arange(fine) // ROWS % N_MEMBER
    pick = jax.random.randint(key, (fine, OFFD), 0, 3)
    steps = jnp.where(pick == 0, N_MEMBER - 1, jnp.where(pick == 1, 1, N_MEMBER // 2))
    sender = (member_idx[:, None] + steps) % N_MEMBER
    within = jax.random.randint(jax.random.fold_in(key, 3), (fine, OFFD), 0, SEND)
    return (sender * SEND + within).astype(jnp.int32)


def draw_p_cols(key, part):
    fine = ROWS * N_GROUP * N_MEMBER
    device_idx = jnp.arange(fine) // ROWS
    member_idx = device_idx % N_MEMBER
    group_idx = device_idx // N_MEMBER
    omit = jax.random.randint(key, (fine,), 0, 3)
    flip = jax.random.randint(jax.random.fold_in(key, 5), (fine,), 0, 2)
    first_kind = jnp.where(omit == 0, 1, 0)
    second_kind = jnp.where(omit == 2, 1, 2)
    lead = jnp.where(flip == 0, first_kind, second_kind)
    trail = jnp.where(flip == 0, second_kind, first_kind)

    def offset(kind):
        return jnp.where(kind == 0, 0, jnp.where(kind == 1, 1, N_GROUP // 2))
    col_one = (group_idx + offset(lead)) % N_GROUP * N_MEMBER + member_idx
    col_two = (group_idx + offset(trail)) % N_GROUP * N_MEMBER + member_idx
    return jnp.stack([col_one, col_two], axis=1).astype(jnp.int32)


def draw_coarse_cols(key, part):
    total = N_GROUP * N_MEMBER
    rows_idx = jnp.arange(total)
    group_idx = rows_idx // N_MEMBER
    member_idx = rows_idx % N_MEMBER
    own = [(group_idx + shift) % N_GROUP * N_MEMBER + member_idx for shift in [0, 1, N_GROUP - 1, N_GROUP // 2]]
    candidates = []
    for shift in [N_GROUP - 1, 0, 1, N_GROUP // 2]:
        for step in [N_MEMBER - 1, 1, N_MEMBER // 2]:
            candidates.append((group_idx + shift) % N_GROUP * N_MEMBER + (member_idx + step) % N_MEMBER)
    pool = jnp.stack(candidates, axis=1)
    scores = jax.random.randint(jax.random.fold_in(key, 7), (total, 12), 0, 1 << 20) * 12 + jnp.arange(12)[None, :]
    order = jnp.argsort(scores, axis=1, stable=True)[:, :4]
    chosen = jnp.take_along_axis(pool, order, axis=1)
    return jnp.concatenate([jnp.stack(own, axis=1), chosen], axis=1).astype(jnp.int32)


def touch_ends(entries, stream_key, least, high):
    spot = [jax.random.randint(jax.random.fold_in(stream_key, axis), (), 0, length) for axis, length in enumerate(entries.shape)]
    longest = entries.shape.index(max(entries.shape))
    beside = spot[:longest] + [(spot[longest] + 1) % entries.shape[longest]] + spot[longest + 1:]
    return entries.at[tuple(spot)].set(least).at[tuple(beside)].set(high)


def steps_of(stream_key, dims, shards, smallest, top_value):
    level, own = 1.0, jax.random.fold_in(stream_key, 6)
    for axis_at, shards_of in shards:
        draws = jnp.exp(jax.random.uniform(jax.random.fold_in(own, axis_at), (shards_of,), jnp.float32, smallest / len(shards), top_value / len(shards)))
        level = level * jnp.repeat(draws, dims[axis_at] // shards_of).reshape([-1 if axis == axis_at else 1 for axis in range(len(dims))])
    return level


def normal_values(key, dims, width, bound, shards=(), held_as=jnp.bfloat16):
    level = steps_of(key, dims, shards, -0.22, 0.18) if shards else 1.0
    array = jax.random.normal(key, dims, jnp.float32) * width * level
    return jnp.minimum(jnp.maximum(array, -bound), bound).astype(held_as)


def setup_inputs(seed: int = 0) -> dict:
    key_list = jax.random.split(jax.random.key(seed), 10)
    return {
        "diag_tiles": normal_values(key_list[0], (FINE, DIAG, TILE, TILE), (TILE * (DIAG + OFFD)) ** -0.5, 0.21875, ((0, 256),)),
        "diag_cols": touch_ends(jax.random.randint(key_list[1], (FINE, DIAG), 0, ROWS), jax.random.fold_in(key_list[1], 1), 0, ROWS - 1).astype(jnp.int32),
        "offd_tiles": normal_values(key_list[2], (FINE, OFFD, TILE, TILE), (TILE * (DIAG + OFFD)) ** -0.5, 0.21875, ((0, 256),)),
        "offd_cols": draw_offd_cols(jax.random.fold_in(key_list[9], 71), 0),
        "offd_count": touch_ends(jax.random.randint(key_list[4], (FINE,), 0, OFFD + 1), jax.random.fold_in(key_list[4], 1), 0, OFFD).astype(jnp.int32),
        "p_tiles": normal_values(key_list[5], (FINE, PTILES, TILE, TILE), 0.33, 2.0, ((0, 256),)),
        "p_cols": draw_p_cols(jax.random.fold_in(key_list[9], 71), 0),
        "send_rows": touch_ends(jax.random.randint(key_list[7], (COARSE, MEMBERS, SEND), 0, ROWS), jax.random.fold_in(key_list[7], 1), 0, ROWS - 1).astype(jnp.int32),
        "coarse_cols": draw_coarse_cols(jax.random.fold_in(key_list[9], 71), 0),
    }


def product_terms(a_tiles, p_rows, p_ids, targets, live):
    ap = jnp.einsum('rkab,rkqbc->rkqac', a_tiles.astype(jnp.float32), p_rows.astype(jnp.float32)).astype(jnp.bfloat16)
    match = p_ids[:, None, None, :, :] == targets[:, :, :, None, None]
    match = jnp.logical_and(match, live[:, None, None, :, None])
    return jnp.einsum('rpskq,rkqac->rpsac', match.astype(jnp.float32), ap.astype(jnp.float32))


def reference(diag_tiles, diag_cols, offd_tiles, offd_cols, offd_count, p_tiles, p_cols, send_rows, coarse_cols):
    members = N_MEMBER
    groups = N_GROUP

    def device(index):
        group_idx = index // members
        member_idx = index % members
        base = index * ROWS

        def local(x):
            return lax.dynamic_slice_in_dim(x, base, ROWS, 0)

        senders = (group_idx * members + jnp.arange(members)).astype(jnp.int32)
        picked = send_rows[senders][:, member_idx, :]
        remote = (senders[:, None] * ROWS + picked).reshape(-1).astype(jnp.int32)
        rows_diag = (base + local(diag_cols)).astype(jnp.int32)
        rows_offd = remote[local(offd_cols)]
        own_cols = local(p_cols)
        own_tiles = local(p_tiles)
        targets = coarse_cols[own_cols]
        full_live = jnp.ones((ROWS, DIAG), dtype=bool)
        counted = jnp.arange(OFFD)[None, :] < local(offd_count)[:, None]
        summed = product_terms(local(diag_tiles), p_tiles[rows_diag], p_cols[rows_diag], targets, full_live)
        summed = summed + product_terms(local(offd_tiles), p_tiles[rows_offd], p_cols[rows_offd], targets, counted)
        y_tiles = summed.astype(jnp.bfloat16)
        products = jnp.einsum('rpba,rpsbc->rpsac', own_tiles.astype(jnp.float32), y_tiles.astype(jnp.float32))
        route = (jnp.arange(groups)[:, None, None] == (own_cols // members)[None]).astype(jnp.float32)
        return jnp.einsum('grp,rpsac->gsac', route, products, precision=lax.Precision.HIGHEST).astype(jnp.bfloat16)

    partials = lax.map(device, jnp.arange(groups * members).astype(jnp.int32))

    def add_group(total, grp):
        block = lax.dynamic_slice_in_dim(partials, grp * members, members, 0)
        return total + block.astype(jnp.float32), None

    start = jnp.zeros((members, groups, CTILES, TILE, TILE), jnp.float32)
    total, _ = lax.scan(add_group, start, jnp.arange(groups).astype(jnp.int32))
    return jnp.transpose(total, (1, 0, 2, 3, 4)).reshape(groups * members, CTILES, TILE, TILE)
```

```python
import functools

import jax
import jax.numpy as jnp
from jax import lax
from jax.experimental import pallas as pl
from jax.experimental.pallas import tpu as pltpu
from jax.sharding import PartitionSpec as P


T = 128
HDR = 16
BF = jnp.bfloat16
F32 = jnp.float32


def kind_of(row_group, group, groups):
    rel = lax.rem(row_group - group + groups, groups)
    return jnp.where(rel == 0, 0, jnp.where(rel == 1, 1, jnp.where(rel == groups // 2, 2, 3)))


def partners_of(member, members):
    odd = lax.rem(member, 2)
    up = lax.rem(member + 1, members)
    down = lax.rem(member + members - 1, members)
    return (
        jnp.where(odd == 1, down, up),
        jnp.where(odd == 1, up, down),
        lax.rem(member + members // 2, members),
    )


def pick_kernel(groups, members, send_ref, pc_ref, p_ref, *rest):
    outs, (hdr, sems) = rest[:3], rest[3:]
    group = lax.axis_index("group")
    partners = partners_of(lax.axis_index("member"), members)
    copies = []
    rows = []
    for e in range(3):
        row = send_ref[0, partners[e], 0]
        rows.append(row)
        copy = pltpu.make_async_copy(p_ref.at[row], outs[e].at[pl.ds(0, 2 * T), :], sems.at[e])
        copy.start()
        copies.append(copy)
    for e in range(3):
        for q in range(2):
            kind = kind_of(pc_ref[rows[e], q] // members, group, groups)
            hdr[e, q * 8 : q * 8 + 8, :] = jnp.full((8, T), kind.astype(F32), F32).astype(BF)
        copy = pltpu.make_async_copy(
            hdr.at[e], outs[e].at[pl.ds(2 * T, HDR), :], sems.at[3 + e]
        )
        copies.append(copy)
    for copy in copies[3:]:
        copy.start()
    for copy in copies:
        copy.wait()


def local_kernel(
    groups, members, rows,
    pc_ref, dc_ref, oc_ref, cnt_ref, p_hbm, d_hbm, o_hbm,
    far_ref, near_ref, q_ref,
    pv, dv, ov, pd, pt, aq, zs, psem, dsem, osem,
):
    group = lax.axis_index("group")
    partners = partners_of(lax.axis_index("member"), members)
    chunk = 4
    parts = rows // chunk

    def copy_of(src, dst, sem, c):
        at = pl.ds(c * chunk, chunk)
        return pltpu.make_async_copy(src.at[at], dst.at[at], sem.at[c])

    for src, dst, sem in ((p_hbm, pv, psem), (o_hbm, ov, osem), (d_hbm, dv, dsem)):
        for c in range(parts):
            copy_of(src, dst, sem, c).start()

    zero = jnp.zeros((T, T), BF)
    for c in range(parts):
        copy_of(p_hbm, pv, psem, c).wait()
        for f in range(c * chunk, c * chunk + chunk):
            k0 = kind_of(pc_ref[f, 0] // members, group, groups)
            k1 = kind_of(pc_ref[f, 1] // members, group, groups)
            none = 3 - k0 - k1
            pd[f, none] = zero
            pt[f, none] = zero
            for q, k in ((0, k0), (1, k1)):
                tile = pv[f, q]
                pd[f, k] = tile
                pt[f, k] = tile.T
    for c in range(parts):
        copy_of(o_hbm, ov, osem, c).wait()
        for f in range(c * chunk, c * chunk + chunk):
            for e in range(3):
                aq[f, e] = zero
            for k in range(2):
                sender = oc_ref[f, k]
                e = jnp.where(sender == partners[0], 0, jnp.where(sender == partners[1], 1, 2))
                e = jnp.where(k < cnt_ref[f], e, 3)
                if k == 0:
                    aq[f, e] = ov[f, k]
                else:
                    aq[f, e] = aq[f, e] + ov[f, k]

    def left(h):
        return jnp.concatenate([pt[f, h] for f in range(rows)], axis=1)

    lhs = jnp.concatenate([left(h) for h in range(3)], axis=0)
    rhs = jnp.concatenate(
        [jnp.concatenate([aq[f, e] for e in range(3)], axis=1) for f in range(rows)], axis=0
    )
    qs = jnp.dot(lhs, rhs, preferred_element_type=F32)
    for h in range(3):
        for e in range(3):
            block = qs[h * T : (h + 1) * T, e * T : (e + 1) * T]
            high = block.astype(BF)
            q_ref[h, e, :, 0:T] = high
            q_ref[h, e, :, T : 2 * T] = (block - high.astype(F32)).astype(BF)

    for c in range(parts):
        copy_of(d_hbm, dv, dsem, c).wait()
        for f in range(c * chunk, c * chunk + chunk):
            a = jnp.concatenate([dv[f, k] for k in range(4)], axis=1)
            js = [dc_ref[f, k] for k in range(4)]
            b = jnp.concatenate(
                [jnp.concatenate([pd[j, h] for h in range(3)], axis=1) for j in js], axis=0
            )
            zs[f * T : (f + 1) * T, :] = jnp.dot(a, b, preferred_element_type=F32).astype(BF)
    gs = jnp.dot(lhs, zs[...], preferred_element_type=F32)

    def tile_of(h, c):
        return gs[h * T : (h + 1) * T, c * T : (c + 1) * T]

    for i, (h, c) in enumerate(((1, 1), (1, 0), (2, 2), (2, 0))):
        far_ref[i] = tile_of(h, c).astype(BF)
    for c in range(3):
        near_ref[c] = tile_of(0, c)


def received(pay_refs, rd):
    for e in range(3):
        kinds = [
            jnp.broadcast_to(pay_refs[e][2 * T + 8 * q : 2 * T + 8 * q + 1, :].astype(F32), (T, T))
            for q in range(2)
        ]
        tiles = [pay_refs[e][q * T : (q + 1) * T, :].astype(F32) for q in range(2)]
        for h in range(3):
            tile = jnp.where(
                kinds[0] == h, tiles[0], jnp.where(kinds[1] == h, tiles[1], 0.0)
            ).astype(BF)
            rd[e, h, 0:T, :] = tile
            rd[e, h, T : 2 * T, :] = tile
        rd[e, 3] = jnp.zeros((2 * T, T), BF)


def remote_tile(groups, members, group, partners, cc_ref, q_ref, rd, h, s):
    row = lax.rem(group + (0, 1, groups // 2)[h], groups) * members + lax.axis_index("member")
    col = cc_ref[row, 4 + s]
    m2 = lax.rem(col, members)
    e = jnp.where(m2 == partners[0], 0, jnp.where(m2 == partners[1], 1, 2))
    kind = kind_of(col // members, group, groups)
    return jnp.dot(q_ref[h, e], rd[e, kind], preferred_element_type=F32)


def far_kernel(groups, members, cc_ref, far_ref, q_ref, r0, r1, r2, s1_ref, s4_ref, rd):
    group = lax.axis_index("group")
    partners = partners_of(lax.axis_index("member"), members)
    received((r0, r1, r2), rd)
    for h, out in ((2, s4_ref), (1, s1_ref)):
        out[0] = far_ref[2 * h - 2]
        out[1] = far_ref[2 * h - 1]
        for s in range(4):
            tile = remote_tile(groups, members, group, partners, cc_ref, q_ref, rd, h, s)
            out[2 + s] = tile.astype(BF)


def near_kernel(groups, members, cc_ref, near_ref, q_ref, r0, r1, r2, own_ref, rd):
    group = lax.axis_index("group")
    partners = partners_of(lax.axis_index("member"), members)
    received((r0, r1, r2), rd)
    own_ref[0] = near_ref[0]
    own_ref[1] = near_ref[1]
    own_ref[2] = jnp.zeros((T, T), F32)
    own_ref[3] = near_ref[2]
    for s in range(4):
        own_ref[4 + s] = remote_tile(groups, members, group, partners, cc_ref, q_ref, rd, 0, s)


def add_kernel(own_ref, a1_ref, a4_ref, out_ref):
    out_ref[0, 0] = own_ref[0] + a1_ref[0].astype(F32) + a4_ref[0].astype(F32)
    out_ref[0, 1] = own_ref[1]
    out_ref[0, 2] = own_ref[2] + a1_ref[1].astype(F32)
    out_ref[0, 3] = own_ref[3] + a4_ref[1].astype(F32)
    for s in range(4):
        out_ref[0, 4 + s] = (
            own_ref[4 + s] + a1_ref[2 + s].astype(F32) + a4_ref[2 + s].astype(F32)
        )


def on_device(
    diag_tiles, diag_cols, offd_tiles, offd_cols, offd_count, p_tiles, p_cols, send_rows,
    coarse_cols,
):
    rows = p_tiles.shape[0]
    groups = lax.axis_size("group")
    members = lax.axis_size("member")
    smem = pl.BlockSpec(memory_space=pltpu.SMEM)
    vmem = pl.BlockSpec(memory_space=pltpu.VMEM)
    hbm = pl.BlockSpec(memory_space=pl.ANY)
    params = pltpu.CompilerParams(vmem_limit_bytes=48 << 20)

    payload = jax.ShapeDtypeStruct((2 * T + HDR, T), BF)
    sends = pl.pallas_call(
        functools.partial(pick_kernel, groups, members),
        out_shape=(payload,) * 3,
        in_specs=[smem, smem, hbm],
        out_specs=(hbm,) * 3,
        scratch_shapes=[pltpu.VMEM((3, HDR, T), BF), pltpu.SemaphoreType.DMA((6,))],
        name="pick",
    )(send_rows, p_cols, p_tiles.reshape(rows, 2 * T, T))
    half = members // 2
    pairs = (
        [(i, i ^ 1) for i in range(members)],
        [(i, (i - 1 if i % 2 == 0 else i + 1) % members) for i in range(members)],
        [(i, (i + half) % members) for i in range(members)],
    )
    got = [lax.ppermute(x, "member", perm) for x, perm in zip(sends, pairs)]

    far, near, qs = pl.pallas_call(
        functools.partial(local_kernel, groups, members, rows),
        out_shape=(
            jax.ShapeDtypeStruct((4, T, T), BF),
            jax.ShapeDtypeStruct((3, T, T), F32),
            jax.ShapeDtypeStruct((3, 3, T, 2 * T), BF),
        ),
        in_specs=[smem] * 4 + [hbm] * 3,
        out_specs=(vmem,) * 3,
        scratch_shapes=[
            pltpu.VMEM((rows, 2, T, T), BF),
            pltpu.VMEM((rows, 4, T, T), BF),
            pltpu.VMEM((rows, 2, T, T), BF),
            pltpu.VMEM((rows, 3, T, T), BF),
            pltpu.VMEM((rows, 3, T, T), BF),
            pltpu.VMEM((rows, 4, T, T), BF),
            pltpu.VMEM((rows * T, 3 * T), BF),
            pltpu.SemaphoreType.DMA((4,)),
            pltpu.SemaphoreType.DMA((4,)),
            pltpu.SemaphoreType.DMA((4,)),
        ],
        compiler_params=params,
        name="local",
    )(p_cols, diag_cols, offd_cols, offd_count, p_tiles, diag_tiles, offd_tiles)

    rd = pltpu.VMEM((3, 4, 2 * T, T), BF)
    six = jax.ShapeDtypeStruct((6, T, T), BF)
    send1, send4 = pl.pallas_call(
        functools.partial(far_kernel, groups, members),
        out_shape=(six, six),
        in_specs=[smem] + [vmem] * 5,
        out_specs=(vmem, vmem),
        scratch_shapes=[rd],
        name="far",
    )(coarse_cols, far, qs, *got)
    shift = groups // 2
    arrived4 = lax.ppermute(send4, "group", [(i, (i + shift) % groups) for i in range(groups)])
    arrived1 = lax.ppermute(send1, "group", [(i, (i + 1) % groups) for i in range(groups)])
    own = pl.pallas_call(
        functools.partial(near_kernel, groups, members),
        out_shape=jax.ShapeDtypeStruct((8, T, T), F32),
        in_specs=[smem] + [vmem] * 5,
        out_specs=vmem,
        scratch_shapes=[rd],
        name="near",
    )(coarse_cols, near, qs, *got)
    return pl.pallas_call(
        add_kernel,
        out_shape=jax.ShapeDtypeStruct((1, 8, T, T), F32),
        in_specs=[vmem] * 3,
        out_specs=vmem,
        name="add",
    )(own, arrived1, arrived4)


def solution(mesh):
    return jax.shard_map(
        on_device,
        mesh=mesh,
        in_specs=(
            P(("group", "member"), None, None, None),
            P(("group", "member"), None),
            P(("group", "member"), None, None, None),
            P(("group", "member"), None),
            P(("group", "member")),
            P(("group", "member"), None, None, None),
            P(("group", "member"), None),
            P(("group", "member"), None, None),
            P(),
        ),
        out_specs=P(("group", "member"), None, None, None),
        check_vma=False,
    )
```

```python
import functools

import jax
import jax.numpy as jnp
from jax import lax
from jax.experimental import pallas as pl
from jax.experimental.pallas import tpu as pltpu
from jax.sharding import PartitionSpec as P


T = 128
HDR = 16
BF = jnp.bfloat16
F32 = jnp.float32


def kind_of(row_group, group, groups):
    rel = lax.rem(row_group - group + groups, groups)
    return jnp.where(rel == 0, 0, jnp.where(rel == 1, 1, jnp.where(rel == groups // 2, 2, 3)))


def partners_of(member, members):
    odd = lax.rem(member, 2)
    up = lax.rem(member + 1, members)
    down = lax.rem(member + members - 1, members)
    return (
        jnp.where(odd == 1, down, up),
        jnp.where(odd == 1, up, down),
        lax.rem(member + members // 2, members),
    )


def pick_kernel(groups, members, send_hbm, pc_hbm, p_hbm, o0, o1, o2, pv, send_ref, pc_ref, sems):
    group = lax.axis_index("group")
    partners = partners_of(lax.axis_index("member"), members)
    copies = [
        pltpu.make_async_copy(send_hbm, send_ref, sems.at[0]),
        pltpu.make_async_copy(pc_hbm, pc_ref, sems.at[1]),
        pltpu.make_async_copy(p_hbm, pv, sems.at[2]),
    ]
    for copy in copies:
        copy.start()
    copies[0].wait()
    copies[1].wait()
    rows = [send_ref[0, partner] for partner in partners]
    for row, out in zip(rows, (o0, o1, o2)):
        for q in range(2):
            kind = kind_of(pc_ref[q, row] // members, group, groups)
            at = 2 * T + q * (HDR // 2)
            out[at : at + HDR // 2, :] = jnp.full((HDR // 2, T), kind.astype(F32), F32).astype(BF)
    copies[2].wait()
    for row, out in zip(rows, (o0, o1, o2)):
        out[0:T, :] = pv[row, 0]
        out[T : 2 * T, :] = pv[row, 1]


def local_kernel(
    groups, members, rows,
    pc_hbm, dc_hbm, oc_hbm, cnt_hbm, pv, d_hbm, o_hbm,
    far_ref, near_ref, q_ref,
    pc_ref, dc_ref, oc_ref, cnt_ref, dv, ov, pd, pt, aq, zs, ssem, dsem, osem,
):
    group = lax.axis_index("group")
    partners = partners_of(lax.axis_index("member"), members)
    chunk = 4
    parts = rows // chunk

    def copy_of(src, dst, sem, c):
        at = pl.ds(c * chunk, chunk)
        return pltpu.make_async_copy(src.at[at], dst.at[at], sem.at[c])

    small = [
        pltpu.make_async_copy(src, dst, ssem.at[i])
        for i, (src, dst) in enumerate(
            ((pc_hbm, pc_ref), (oc_hbm, oc_ref), (cnt_hbm, cnt_ref), (dc_hbm, dc_ref))
        )
    ]
    for copy in small:
        copy.start()
    for src, dst, sem in ((o_hbm, ov, osem), (d_hbm, dv, dsem)):
        for c in range(parts):
            copy_of(src, dst, sem, c).start()
    for copy in small:
        copy.wait()

    zero = jnp.zeros((T, T), BF)
    for f in range(rows):
        k0 = kind_of(pc_ref[0, f] // members, group, groups)
        k1 = kind_of(pc_ref[1, f] // members, group, groups)
        none = 3 - k0 - k1
        pd[f, none] = zero
        pt[f, none] = zero
        for q, k in ((0, k0), (1, k1)):
            tile = pv[f, q]
            pd[f, k] = tile
            pt[f, k] = tile.T
    for c in range(parts):
        copy_of(o_hbm, ov, osem, c).wait()
        for f in range(c * chunk, c * chunk + chunk):
            for e in range(3):
                aq[f, e] = zero
            for k in range(2):
                sender = oc_ref[k, f]
                e = jnp.where(sender == partners[0], 0, jnp.where(sender == partners[1], 1, 2))
                e = jnp.where(k < cnt_ref[f], e, 3)
                if k == 0:
                    aq[f, e] = ov[f, k]
                else:
                    aq[f, e] = aq[f, e] + ov[f, k]

    def left(h):
        return jnp.concatenate([pt[f, h] for f in range(rows)], axis=1)

    lhs = jnp.concatenate([left(h) for h in range(3)], axis=0)
    rhs = jnp.concatenate(
        [jnp.concatenate([aq[f, e] for e in range(3)], axis=1) for f in range(rows)], axis=0
    )
    qs = jnp.dot(lhs, rhs, preferred_element_type=F32)
    for h in range(3):
        for e in range(3):
            block = qs[h * T : (h + 1) * T, e * T : (e + 1) * T]
            high = block.astype(BF)
            q_ref[h, e, :, 0:T] = high
            q_ref[h, e, :, T : 2 * T] = (block - high.astype(F32)).astype(BF)

    for c in range(parts):
        copy_of(d_hbm, dv, dsem, c).wait()
        for f in range(c * chunk, c * chunk + chunk):
            a = jnp.concatenate([dv[f, k] for k in range(4)], axis=1)
            js = [dc_ref[k, f] for k in range(4)]
            b = jnp.concatenate(
                [jnp.concatenate([pd[j, h] for h in range(3)], axis=1) for j in js], axis=0
            )
            zs[f * T : (f + 1) * T, :] = jnp.dot(a, b, preferred_element_type=F32).astype(BF)
    gs = jnp.dot(lhs, zs[...], preferred_element_type=F32)

    def tile_of(h, c):
        return gs[h * T : (h + 1) * T, c * T : (c + 1) * T]

    for i, (h, c) in enumerate(((1, 1), (1, 0), (2, 2), (2, 0))):
        far_ref[i] = tile_of(h, c).astype(BF)
    for c in range(3):
        near_ref[c] = tile_of(0, c)


def received(pay_refs, rd):
    for e in range(3):
        kinds = [
            jnp.broadcast_to(pay_refs[e][2 * T + 8 * q : 2 * T + 8 * q + 1, :].astype(F32), (T, T))
            for q in range(2)
        ]
        tiles = [pay_refs[e][q * T : (q + 1) * T, :].astype(F32) for q in range(2)]
        for h in range(3):
            tile = jnp.where(
                kinds[0] == h, tiles[0], jnp.where(kinds[1] == h, tiles[1], 0.0)
            ).astype(BF)
            rd[e, h, 0:T, :] = tile
            rd[e, h, T : 2 * T, :] = tile
        rd[e, 3] = jnp.zeros((2 * T, T), BF)


def remote_tile(groups, members, group, partners, cc_ref, q_ref, rd, h, s):
    row = lax.rem(group + (0, 1, groups // 2)[h], groups) * members + lax.axis_index("member")
    col = cc_ref[4 + s, row]
    m2 = lax.rem(col, members)
    e = jnp.where(m2 == partners[0], 0, jnp.where(m2 == partners[1], 1, 2))
    kind = kind_of(col // members, group, groups)
    return jnp.dot(q_ref[h, e], rd[e, kind], preferred_element_type=F32)


def far_kernel(groups, members, cc_ref, far_ref, q_ref, r0, r1, r2, s1_ref, s4_ref, rd):
    group = lax.axis_index("group")
    partners = partners_of(lax.axis_index("member"), members)
    received((r0, r1, r2), rd)
    for h, out in ((2, s4_ref), (1, s1_ref)):
        out[0] = far_ref[2 * h - 2]
        out[1] = far_ref[2 * h - 1]
        for s in range(4):
            tile = remote_tile(groups, members, group, partners, cc_ref, q_ref, rd, h, s)
            out[2 + s] = tile.astype(BF)


def near_kernel(groups, members, cc_ref, near_ref, q_ref, r0, r1, r2, own_ref, rd):
    group = lax.axis_index("group")
    partners = partners_of(lax.axis_index("member"), members)
    received((r0, r1, r2), rd)
    own_ref[0] = near_ref[0]
    own_ref[1] = near_ref[1]
    own_ref[2] = jnp.zeros((T, T), F32)
    own_ref[3] = near_ref[2]
    for s in range(4):
        own_ref[4 + s] = remote_tile(groups, members, group, partners, cc_ref, q_ref, rd, 0, s)


def add_kernel(own_ref, a1_ref, a4_ref, out_ref):
    out_ref[0, 0] = own_ref[0] + a1_ref[0].astype(F32) + a4_ref[0].astype(F32)
    out_ref[0, 1] = own_ref[1]
    out_ref[0, 2] = own_ref[2] + a1_ref[1].astype(F32)
    out_ref[0, 3] = own_ref[3] + a4_ref[1].astype(F32)
    for s in range(4):
        out_ref[0, 4 + s] = (
            own_ref[4 + s] + a1_ref[2 + s].astype(F32) + a4_ref[2 + s].astype(F32)
        )


def on_device(
    diag_tiles, diag_cols, offd_tiles, offd_cols, offd_count, p_tiles, p_cols, send_rows,
    coarse_cols,
):
    rows = p_tiles.shape[0]
    groups = lax.axis_size("group")
    members = lax.axis_size("member")
    vmem = pl.BlockSpec(memory_space=pltpu.VMEM)
    smem = pl.BlockSpec(memory_space=pltpu.SMEM)
    hbm = pl.BlockSpec(memory_space=pl.ANY)
    half = members // 2
    shift = groups // 2

    def inside(x):
        return pltpu.with_memory_space_constraint(x, pltpu.VMEM)

    def outside(x):
        return pltpu.with_memory_space_constraint(x, pltpu.HBM)

    def call(kernel, out_shape, in_specs, scratch, mib, name):
        return pl.pallas_call(
            kernel,
            out_shape=out_shape,
            in_specs=in_specs,
            out_specs=jax.tree.map(
                lambda _: vmem, out_shape, is_leaf=lambda x: not isinstance(x, tuple)
            ),
            scratch_shapes=scratch,
            compiler_params=pltpu.CompilerParams(vmem_limit_bytes=mib << 20),
            name=name,
        )

    pcols = outside(p_cols.T)
    payload = pltpu.VMEM((2 * T + HDR, T), BF)
    *sends, pv = call(
        functools.partial(pick_kernel, groups, members),
        (payload, payload, payload, pltpu.VMEM((rows, 2, T, T), BF)),
        [hbm] * 3,
        [
            pltpu.SMEM((1, members), jnp.int32),
            pltpu.SMEM((2, rows), jnp.int32),
            pltpu.SemaphoreType.DMA((3,)),
        ],
        8,
        "pick",
    )(outside(send_rows.reshape(1, members)), pcols, outside(p_tiles))
    pairs = (
        [(i, (i - 1 if i % 2 == 0 else i + 1) % members) for i in range(members)],
        [(i, (i + half) % members) for i in range(members)],
        [(i, i ^ 1) for i in range(members)],
    )
    r1 = lax.ppermute(sends[1], "member", pairs[0])
    r2 = lax.ppermute(sends[2], "member", pairs[1])
    r0 = lax.ppermute(sends[0], "member", pairs[2])
    got = [inside(x) for x in (r0, r1, r2)]

    far, near, qs = call(
        functools.partial(local_kernel, groups, members, rows),
        (
            pltpu.VMEM((4, T, T), BF),
            pltpu.VMEM((3, T, T), F32),
            pltpu.VMEM((3, 3, T, 2 * T), BF),
        ),
        [hbm] * 4 + [vmem] + [hbm] * 2,
        [
            pltpu.SMEM((2, rows), jnp.int32),
            pltpu.SMEM((4, rows), jnp.int32),
            pltpu.SMEM((2, rows), jnp.int32),
            pltpu.SMEM((rows,), jnp.int32),
            pltpu.VMEM((rows, 4, T, T), BF),
            pltpu.VMEM((rows, 2, T, T), BF),
            pltpu.VMEM((rows, 3, T, T), BF),
            pltpu.VMEM((rows, 3, T, T), BF),
            pltpu.VMEM((rows, 4, T, T), BF),
            pltpu.VMEM((rows * T, 3 * T), BF),
            pltpu.SemaphoreType.DMA((4,)),
            pltpu.SemaphoreType.DMA((4,)),
            pltpu.SemaphoreType.DMA((4,)),
        ],
        32,
        "local",
    )(
        pcols, outside(diag_cols.T), outside(offd_cols.T), outside(offd_count),
        inside(pv), outside(diag_tiles), outside(offd_tiles),
    )
    far, near, qs = inside(far), inside(near), inside(qs)

    rd = pltpu.VMEM((3, 4, 2 * T, T), BF)
    six = pltpu.VMEM((6, T, T), BF)
    ccols = outside(coarse_cols.T)
    send1, send4 = call(
        functools.partial(far_kernel, groups, members),
        (six, six), [smem] + [vmem] * 5, [rd], 8, "far",
    )(ccols, far, qs, *got)
    arrived4 = lax.ppermute(send4, "group", [(i, (i + shift) % groups) for i in range(groups)])
    arrived1 = lax.ppermute(send1, "group", [(i, (i + 1) % groups) for i in range(groups)])
    own = call(
        functools.partial(near_kernel, groups, members),
        pltpu.VMEM((8, T, T), F32), [smem] + [vmem] * 5, [rd], 8, "near",
    )(ccols, near, qs, *got)
    return pl.pallas_call(
        add_kernel,
        out_shape=jax.ShapeDtypeStruct((1, 8, T, T), F32),
        in_specs=[vmem] * 3,
        out_specs=vmem,
        compiler_params=pltpu.CompilerParams(vmem_limit_bytes=8 << 20),
        name="add",
    )(inside(own), inside(arrived1), inside(arrived4))


def solution(mesh):
    return jax.shard_map(
        on_device,
        mesh=mesh,
        in_specs=(
            P(("group", "member"), None, None, None),
            P(("group", "member"), None),
            P(("group", "member"), None, None, None),
            P(("group", "member"), None),
            P(("group", "member")),
            P(("group", "member"), None, None, None),
            P(("group", "member"), None),
            P(("group", "member"), None, None),
            P(),
        ),
        out_specs=P(("group", "member"), None, None, None),
        check_vma=False,
    )
```

```python
import functools

import jax
import jax.numpy as jnp
from jax import lax
from jax.experimental import pallas as pl
from jax.experimental.pallas import tpu as pltpu
from jax.sharding import PartitionSpec as P


T = 128
HDR = 32
BF = jnp.bfloat16
F32 = jnp.float32


def distance(column, group, groups, members):
    return ((column >> (members.bit_length() - 1)) - group) & (groups - 1)


def kind_of(column, group, groups, members):
    rel = distance(column, group, groups, members)
    return jnp.where(rel < 2, rel, jnp.where(rel == groups // 2, 2, 3))


def live_kind_of(column, group, groups, members):
    return jnp.minimum(distance(column, group, groups, members), 2)


def partners_of(member, members):
    odd = lax.rem(member, 2)
    up = lax.rem(member + 1, members)
    down = lax.rem(member + members - 1, members)
    return (
        jnp.where(odd == 1, down, up),
        jnp.where(odd == 1, up, down),
        lax.rem(member + members // 2, members),
    )


def fill_slots(slot_ref, pc_ref, rows, group, groups, members):
    for f in range(rows):
        for h in range(3):
            slot_ref[h, f] = 2 * rows
    for f in range(rows):
        for q in range(2):
            slot_ref[live_kind_of(pc_ref[q, f], group, groups, members), f] = 2 * f + q


def pick_kernel(
    groups, members, rows,
    send_hbm, pc_hbm, oc_hbm, cnt_hbm, dc_hbm, p_hbm,
    o0, o1, o2, pv, slot_ref, live_ref, dc_out,
    send_ref, pc_ref, oc_ref, cnt_ref, dc_ref, sems,
):
    group = lax.axis_index("group")
    partners = partners_of(lax.axis_index("member"), members)
    copies = [
        pltpu.make_async_copy(src, dst, sems.at[i])
        for i, (src, dst) in enumerate(
            (
                (send_hbm, send_ref),
                (pc_hbm, pc_ref),
                (p_hbm, pv.at[pl.ds(0, 2 * rows)]),
                (oc_hbm, oc_ref),
                (cnt_hbm, cnt_ref),
                (dc_hbm, dc_ref),
            )
        )
    ]
    for copy in copies:
        copy.start()
    pv[2 * rows] = jnp.zeros((T, T), BF)
    copies[0].wait()
    copies[1].wait()
    picked = [send_ref[0, partner] for partner in partners]
    for row, out in zip(picked, (o0, o1, o2)):
        for q in range(2):
            kind = live_kind_of(pc_ref[q, row], group, groups, members)
            at = 2 * T + q * (HDR // 2)
            out[at : at + HDR // 2, :] = jnp.full((HDR // 2, T), kind.astype(F32), F32).astype(BF)
    for copy in copies[3:]:
        copy.wait()
    fill_slots(slot_ref, pc_ref, rows, group, groups, members)
    for f in range(rows):
        for k in range(2):
            sender = oc_ref[k, f]
            e = jnp.where(sender == partners[0], 0, jnp.where(sender == partners[1], 1, 2))
            live_ref[k, f] = jnp.where(k < cnt_ref[f], e, 3)
        for k in range(4):
            dc_out[k, f] = dc_ref[k, f]
    copies[2].wait()
    for row, out in zip(picked, (o0, o1, o2)):
        out[0:T, :] = pv[2 * row]
        out[T : 2 * T, :] = pv[2 * row + 1]


def left_rows(pt, slot_ref, rows, h):
    return jnp.concatenate([pt[slot_ref[h, f]] for f in range(rows)], axis=1)


def remote_right(rows, aq):
    return jnp.concatenate(
        [jnp.concatenate([aq[f, e] for e in range(3)], axis=1) for f in range(rows)], axis=0
    )


def local_right(rows, z):
    return jnp.concatenate([z[f] for f in range(rows)], axis=0)


def split_into(out, qs):
    for e in range(3):
        block = qs[:, e * T : (e + 1) * T]
        high = block.astype(BF)
        out[e, :, 0:T] = high
        out[e, :, T : 2 * T] = (block - high.astype(F32)).astype(BF)


def local_kernel(rows, slot_ref, live_ref, dc_ref, pv, ov, dv, far_ref, q_ref, pt, aq, z):
    zero = jnp.zeros((T, T), BF)
    pt[2 * rows] = zero
    for t in range(2 * rows):
        pt[t] = pv[t].T
    for f in range(rows):
        a = jnp.concatenate([dv[f, k] for k in range(4)], axis=1)
        js = [dc_ref[k, f] for k in range(4)]
        b = jnp.concatenate(
            [jnp.concatenate([pv[slot_ref[h, j]] for h in range(3)], axis=1) for j in js], axis=0
        )
        z[f] = jnp.dot(a, b, preferred_element_type=F32).astype(BF)
        for e in range(3):
            aq[f, e] = lax.select(live_ref[0, f] == e, ov[f, 0], zero) + lax.select(
                live_ref[1, f] == e, ov[f, 1], zero
            )
    lhs = jnp.concatenate([left_rows(pt, slot_ref, rows, h) for h in (1, 2)], axis=0)
    qs = jnp.dot(lhs, remote_right(rows, aq), preferred_element_type=F32)
    gs = jnp.dot(lhs, local_right(rows, z), preferred_element_type=F32).astype(BF)
    for i in range(2):
        split_into(q_ref.at[i], qs[i * T : (i + 1) * T])
    for i, (h, c) in enumerate(((1, 1), (1, 0), (2, 2), (2, 0))):
        far_ref[i] = gs[(h - 1) * T : h * T, c * T : (c + 1) * T]


def received(pay_refs, rd):
    for e in range(3):
        kinds = [pay_refs[e][2 * T + 16 * q : 2 * T + 16 * q + 16, :].astype(F32) for q in range(2)]
        tiles = [pay_refs[e][q * T : (q + 1) * T, :].reshape(8, 16, T) for q in range(2)]
        for h in range(3):
            masks = [jnp.where(kind == h, 1.0, 0.0).astype(BF)[None] for kind in kinds]
            rd[3 * e + h] = (tiles[0] * masks[0] + tiles[1] * masks[1]).reshape(T, T)
    rd[9] = jnp.zeros((T, T), BF)


def remote_tile(groups, members, group, partners, cc_ref, left, rd, h, s):
    row = lax.rem(group + (0, 1, groups // 2)[h], groups) * members + lax.axis_index("member")
    col = cc_ref[4 + s, row]
    m2 = lax.rem(col, members)
    e = jnp.where(m2 == partners[0], 0, jnp.where(m2 == partners[1], 1, 2))
    kind = kind_of(col, group, groups, members)
    tile = rd[jnp.where(kind == 3, 9, 3 * e + kind)]
    return jnp.dot(left[e], jnp.concatenate([tile, tile], axis=0), preferred_element_type=F32)


def far_kernel(groups, members, cc_ref, far_ref, q_ref, r0, r1, r2, s1_ref, s4_ref, rd):
    group = lax.axis_index("group")
    partners = partners_of(lax.axis_index("member"), members)
    received((r0, r1, r2), rd)
    for h, out in ((2, s4_ref), (1, s1_ref)):
        out[0] = far_ref[2 * h - 2]
        out[1] = far_ref[2 * h - 1]
        for s in range(4):
            tile = remote_tile(
                groups, members, group, partners, cc_ref, q_ref.at[h - 1], rd, h, s
            )
            out[2 + s] = tile.astype(BF)


def near_kernel(
    groups, members, rows, cc_ref, slot_ref, pt, aq, z, r0, r1, r2, own_ref, rd, q_ref
):
    group = lax.axis_index("group")
    partners = partners_of(lax.axis_index("member"), members)
    received((r0, r1, r2), rd)
    lhs = left_rows(pt, slot_ref, rows, 0)
    split_into(q_ref, jnp.dot(lhs, remote_right(rows, aq), preferred_element_type=F32))
    near = jnp.dot(lhs, local_right(rows, z), preferred_element_type=F32)
    own_ref[0] = near[:, 0:T]
    own_ref[1] = near[:, T : 2 * T]
    own_ref[2] = jnp.zeros((T, T), F32)
    own_ref[3] = near[:, 2 * T : 3 * T]
    for s in range(4):
        own_ref[4 + s] = remote_tile(groups, members, group, partners, cc_ref, q_ref, rd, 0, s)


def add_kernel(own_ref, a1_ref, a4_ref, out_ref):
    out_ref[0, 0] = own_ref[0] + a1_ref[0].astype(F32) + a4_ref[0].astype(F32)
    out_ref[0, 1] = own_ref[1]
    out_ref[0, 2] = own_ref[2] + a1_ref[1].astype(F32)
    out_ref[0, 3] = own_ref[3] + a4_ref[1].astype(F32)
    for s in range(4):
        out_ref[0, 4 + s] = (
            own_ref[4 + s] + a1_ref[2 + s].astype(F32) + a4_ref[2 + s].astype(F32)
        )


def on_device(
    diag_tiles, diag_cols, offd_tiles, offd_cols, offd_count, p_tiles, p_cols, send_rows,
    coarse_cols,
):
    rows = p_tiles.shape[0]
    groups = lax.axis_size("group")
    members = lax.axis_size("member")
    vmem = pl.BlockSpec(memory_space=pltpu.VMEM)
    smem = pl.BlockSpec(memory_space=pltpu.SMEM)
    hbm = pl.BlockSpec(memory_space=pl.ANY)
    half = members // 2
    shift = groups // 2

    def inside(x):
        return pltpu.with_memory_space_constraint(x, pltpu.VMEM)

    def outside(x):
        return pltpu.with_memory_space_constraint(x, pltpu.HBM)

    def call(kernel, out_shape, in_specs, scratch, mib, mflop=10):
        return pl.pallas_call(
            kernel,
            out_shape=out_shape,
            in_specs=in_specs,
            out_specs=jax.tree.map(
                lambda x: pl.BlockSpec(memory_space=x.memory_space),
                out_shape,
                is_leaf=lambda x: not isinstance(x, tuple),
            ),
            scratch_shapes=scratch,
            compiler_params=pltpu.CompilerParams(vmem_limit_bytes=mib << 20),
            cost_estimate=pl.CostEstimate(
                flops=mflop * 10**6, transcendentals=0, bytes_accessed=mflop * 10**4
            ),
        )

    payload = pltpu.VMEM((2 * T + HDR, T), BF)
    *sends, pv, slot, live, dcols = call(
        functools.partial(pick_kernel, groups, members, rows),
        (
            payload, payload, payload, pltpu.VMEM((2 * rows + 1, T, T), BF),
            pltpu.SMEM((3, rows), jnp.int32),
            pltpu.SMEM((2, rows), jnp.int32),
            pltpu.SMEM((4, rows), jnp.int32),
        ),
        [hbm] * 6,
        [
            pltpu.SMEM((1, members), jnp.int32),
            pltpu.SMEM((2, rows), jnp.int32),
            pltpu.SMEM((2, rows), jnp.int32),
            pltpu.SMEM((rows,), jnp.int32),
            pltpu.SMEM((4, rows), jnp.int32),
            pltpu.SemaphoreType.DMA((6,)),
        ],
        8,
        2000,
    )(
        outside(send_rows.reshape(1, members)), outside(p_cols.T), outside(offd_cols.T),
        outside(offd_count), outside(diag_cols.T), outside(p_tiles.reshape(2 * rows, T, T)),
    )
    pairs = (
        [(i, i ^ 1) for i in range(members)],
        [(i, (i - 1 if i % 2 == 0 else i + 1) % members) for i in range(members)],
        [(i, (i + half) % members) for i in range(members)],
    )
    got = [None] * 3
    for e in (2, 1, 0):
        got[e] = inside(lax.ppermute(sends[e], "member", pairs[e]))

    far, qs, pt, aq, z = call(
        functools.partial(local_kernel, rows),
        (
            pltpu.VMEM((4, T, T), BF),
            pltpu.VMEM((2, 3, T, 2 * T), BF),
            pltpu.VMEM((2 * rows + 1, T, T), BF),
            pltpu.VMEM((rows, 3, T, T), BF),
            pltpu.VMEM((rows, T, 3 * T), BF),
        ),
        [smem] * 3 + [vmem] * 3,
        [],
        16,
        2000,
    )(slot, live, dcols, inside(pv), inside(offd_tiles), inside(diag_tiles))
    far, qs, pt, aq, z = [inside(x) for x in (far, qs, pt, aq, z)]

    def along_group(x, step):
        return inside(lax.ppermute(x, "group", [(i, (i + step) % groups) for i in range(groups)]))

    rd = pltpu.VMEM((10, T, T), BF)
    six = pltpu.VMEM((6, T, T), BF)
    ccols = outside(coarse_cols.T)
    send1, send4 = call(
        functools.partial(far_kernel, groups, members),
        (six, six), [smem] + [vmem] * 5, [rd], 8,
    )(ccols, far, qs, *got)
    a4 = along_group(send4, shift)
    a1 = along_group(send1, 1)
    own = call(
        functools.partial(near_kernel, groups, members, rows),
        pltpu.VMEM((8, T, T), F32), [smem] * 2 + [vmem] * 6,
        [rd, pltpu.VMEM((3, T, 2 * T), BF)], 12, 1000,
    )(ccols, slot, pt, aq, z, *got)
    return pl.pallas_call(
        add_kernel,
        out_shape=jax.ShapeDtypeStruct((1, 8, T, T), F32),
        in_specs=[vmem] * 3,
        out_specs=vmem,
        compiler_params=pltpu.CompilerParams(vmem_limit_bytes=8 << 20),
        name="add",
    )(inside(own), a1, a4)


def solution(mesh):
    return jax.shard_map(
        on_device,
        mesh=mesh,
        in_specs=(
            P(("group", "member"), None, None, None),
            P(("group", "member"), None),
            P(("group", "member"), None, None, None),
            P(("group", "member"), None),
            P(("group", "member")),
            P(("group", "member"), None, None, None),
            P(("group", "member"), None),
            P(("group", "member"), None, None),
            P(),
        ),
        out_specs=P(("group", "member"), None, None, None),
        check_vma=False,
    )
```

```python
import functools

import jax
import jax.numpy as jnp
from jax import lax
from jax.experimental import pallas as pl
from jax.experimental.pallas import tpu as pltpu
from jax.sharding import PartitionSpec as P


T = 128
HDR = 32
BF = jnp.bfloat16
F32 = jnp.float32


def distance(column, group, groups, members):
    return ((column >> (members.bit_length() - 1)) - group) & (groups - 1)


def kind_of(column, group, groups, members):
    rel = distance(column, group, groups, members)
    return jnp.where(rel < 2, rel, jnp.where(rel == groups // 2, 2, 3))


def live_kind_of(column, group, groups, members):
    return jnp.minimum(distance(column, group, groups, members), 2)


def partners_of(member, members):
    odd = lax.rem(member, 2)
    up = lax.rem(member + 1, members)
    down = lax.rem(member + members - 1, members)
    return (
        jnp.where(odd == 1, down, up),
        jnp.where(odd == 1, up, down),
        lax.rem(member + members // 2, members),
    )


def fill_slots(slot_ref, pc_ref, rows, group, groups, members):
    for f in range(rows):
        for h in range(3):
            slot_ref[h, f] = 2 * rows
    for f in range(rows):
        for q in range(2):
            slot_ref[live_kind_of(pc_ref[q, f], group, groups, members), f] = 2 * f + q


def pick_kernel(
    groups, members, rows,
    send_hbm, pc_hbm, oc_hbm, cnt_hbm, dc_hbm, cc_hbm, p_hbm,
    o0, o1, o2, pv, slot_ref, live_ref, dc_out, pick_ref,
    send_ref, pc_ref, oc_ref, cnt_ref, dc_ref, cc_ref, sems,
):
    group = lax.axis_index("group")
    partners = partners_of(lax.axis_index("member"), members)
    copies = [
        pltpu.make_async_copy(src, dst, sems.at[i])
        for i, (src, dst) in enumerate(
            (
                (send_hbm, send_ref),
                (pc_hbm, pc_ref),
                (p_hbm, pv.at[pl.ds(0, 2 * rows)]),
                (oc_hbm, oc_ref),
                (cnt_hbm, cnt_ref),
                (dc_hbm, dc_ref),
                (cc_hbm, cc_ref),
            )
        )
    ]
    for copy in copies:
        copy.start()
    pv[2 * rows] = jnp.zeros((T, T), BF)
    copies[0].wait()
    copies[1].wait()
    picked = [send_ref[0, partner] for partner in partners]
    for row, out in zip(picked, (o0, o1, o2)):
        for q in range(2):
            kind = live_kind_of(pc_ref[q, row], group, groups, members)
            at = 2 * T + q * (HDR // 2)
            out[at : at + HDR // 2, :] = jnp.full((HDR // 2, T), kind.astype(F32), F32).astype(BF)
    for copy in copies[3:]:
        copy.wait()
    fill_slots(slot_ref, pc_ref, rows, group, groups, members)
    for f in range(rows):
        for k in range(2):
            sender = oc_ref[k, f]
            e = jnp.where(sender == partners[0], 0, jnp.where(sender == partners[1], 1, 2))
            live_ref[k, f] = jnp.where(k < cnt_ref[f], e, 3)
        for k in range(4):
            dc_out[k, f] = dc_ref[k, f]
    for h in range(3):
        target = ((group + (0, 1, groups // 2)[h]) & (groups - 1)) * members
        for s in range(4):
            col = cc_ref[4 + s, target + lax.axis_index("member")]
            m2 = col & (members - 1)
            e = jnp.where(m2 == partners[0], 0, jnp.where(m2 == partners[1], 1, 2))
            kind = kind_of(col, group, groups, members)
            pick_ref[2 * h, s] = e
            pick_ref[2 * h + 1, s] = jnp.where(kind == 3, 9, 3 * e + kind)
    copies[2].wait()
    for row, out in zip(picked, (o0, o1, o2)):
        out[0:T, :] = pv[2 * row]
        out[T : 2 * T, :] = pv[2 * row + 1]


def left_rows(pt, slot_ref, rows, h):
    return jnp.concatenate([pt[slot_ref[h, f]] for f in range(rows)], axis=1)


def remote_right(rows, aq):
    return jnp.concatenate(
        [jnp.concatenate([aq[f, e] for e in range(3)], axis=1) for f in range(rows)], axis=0
    )


def local_right(rows, z):
    return jnp.concatenate([z[f] for f in range(rows)], axis=0)


def split_into(out, qs):
    for e in range(3):
        block = qs[:, e * T : (e + 1) * T]
        high = block.astype(BF)
        out[e, :, 0:T] = high
        out[e, :, T : 2 * T] = (block - high.astype(F32)).astype(BF)


def local_kernel(rows, slot_ref, live_ref, dc_ref, pv, ov, dv, far_ref, q_ref, pt, aq, z):
    zero = jnp.zeros((T, T), BF)
    pt[2 * rows] = zero
    for t in range(2 * rows):
        pt[t] = pv[t].T
    for f in range(rows):
        a = jnp.concatenate([dv[f, k] for k in range(4)], axis=1)
        js = [dc_ref[k, f] for k in range(4)]
        b = jnp.concatenate(
            [jnp.concatenate([pv[slot_ref[h, j]] for h in range(3)], axis=1) for j in js], axis=0
        )
        z[f] = jnp.dot(a, b, preferred_element_type=F32).astype(BF)
        for e in range(3):
            aq[f, e] = lax.select(live_ref[0, f] == e, ov[f, 0], zero) + lax.select(
                live_ref[1, f] == e, ov[f, 1], zero
            )
    lhs = jnp.concatenate([left_rows(pt, slot_ref, rows, h) for h in (1, 2)], axis=0)
    qs = jnp.dot(lhs, remote_right(rows, aq), preferred_element_type=F32)
    gs = jnp.dot(lhs, local_right(rows, z), preferred_element_type=F32).astype(BF)
    for i in range(2):
        split_into(q_ref.at[i], qs[i * T : (i + 1) * T])
    for i, (h, c) in enumerate(((1, 1), (1, 0), (2, 2), (2, 0))):
        far_ref[i] = gs[(h - 1) * T : h * T, c * T : (c + 1) * T]


def received(pay_refs, rd):
    for e in range(3):
        kinds = [pay_refs[e][2 * T + 16 * q : 2 * T + 16 * q + 16, :].astype(F32) for q in range(2)]
        tiles = [pay_refs[e][q * T : (q + 1) * T, :].reshape(8, 16, T) for q in range(2)]
        for h in range(3):
            masks = [jnp.where(kind == h, 1.0, 0.0).astype(BF)[None] for kind in kinds]
            rd[3 * e + h] = (tiles[0] * masks[0] + tiles[1] * masks[1]).reshape(T, T)
    rd[9] = jnp.zeros((T, T), BF)


def remote_tile(pick_ref, left, rd, h, s):
    tile = rd[pick_ref[2 * h + 1, s]]
    return jnp.dot(
        left[pick_ref[2 * h, s]],
        jnp.concatenate([tile, tile], axis=0),
        preferred_element_type=F32,
    )


def far_kernel(pick_ref, far_ref, q_ref, r0, r1, r2, s1_ref, s4_ref, rd):
    received((r0, r1, r2), rd)
    for h, out in ((2, s4_ref), (1, s1_ref)):
        out[0] = far_ref[2 * h - 2]
        out[1] = far_ref[2 * h - 1]
        for s in range(4):
            out[2 + s] = remote_tile(pick_ref, q_ref.at[h - 1], rd, h, s).astype(BF)


def near_kernel(rows, pick_ref, slot_ref, pt, aq, z, r0, r1, r2, own_ref, rd, q_ref):
    received((r0, r1, r2), rd)
    lhs = left_rows(pt, slot_ref, rows, 0)
    split_into(q_ref, jnp.dot(lhs, remote_right(rows, aq), preferred_element_type=F32))
    near = jnp.dot(lhs, local_right(rows, z), preferred_element_type=F32)
    own_ref[0] = near[:, 0:T]
    own_ref[1] = near[:, T : 2 * T]
    own_ref[2] = jnp.zeros((T, T), F32)
    own_ref[3] = near[:, 2 * T : 3 * T]
    for s in range(4):
        own_ref[4 + s] = remote_tile(pick_ref, q_ref, rd, 0, s)


def add_kernel(own_ref, a1_ref, a4_ref, out_ref):
    out_ref[0, 0] = own_ref[0] + a1_ref[0].astype(F32) + a4_ref[0].astype(F32)
    out_ref[0, 1] = own_ref[1]
    out_ref[0, 2] = own_ref[2] + a1_ref[1].astype(F32)
    out_ref[0, 3] = own_ref[3] + a4_ref[1].astype(F32)
    for s in range(4):
        out_ref[0, 4 + s] = (
            own_ref[4 + s] + a1_ref[2 + s].astype(F32) + a4_ref[2 + s].astype(F32)
        )


def on_device(
    diag_tiles, diag_cols, offd_tiles, offd_cols, offd_count, p_tiles, p_cols, send_rows,
    coarse_cols,
):
    rows = p_tiles.shape[0]
    groups = lax.axis_size("group")
    members = lax.axis_size("member")
    vmem = pl.BlockSpec(memory_space=pltpu.VMEM)
    smem = pl.BlockSpec(memory_space=pltpu.SMEM)
    hbm = pl.BlockSpec(memory_space=pl.ANY)
    half = members // 2
    shift = groups // 2

    def inside(x):
        return pltpu.with_memory_space_constraint(x, pltpu.VMEM)

    def outside(x):
        return pltpu.with_memory_space_constraint(x, pltpu.HBM)

    def call(kernel, out_shape, in_specs, scratch, mib, mflop=10):
        return pl.pallas_call(
            kernel,
            out_shape=out_shape,
            in_specs=in_specs,
            out_specs=jax.tree.map(
                lambda x: pl.BlockSpec(memory_space=x.memory_space),
                out_shape,
                is_leaf=lambda x: not isinstance(x, tuple),
            ),
            scratch_shapes=scratch,
            compiler_params=pltpu.CompilerParams(vmem_limit_bytes=mib << 20),
            cost_estimate=pl.CostEstimate(
                flops=mflop * 10**6, transcendentals=0, bytes_accessed=mflop * 10**4
            ),
        )

    payload = pltpu.VMEM((2 * T + HDR, T), BF)
    *sends, pv, slot, live, dcols, chosen = call(
        functools.partial(pick_kernel, groups, members, rows),
        (
            payload, payload, payload, pltpu.VMEM((2 * rows + 1, T, T), BF),
            pltpu.SMEM((3, rows), jnp.int32),
            pltpu.SMEM((2, rows), jnp.int32),
            pltpu.SMEM((4, rows), jnp.int32),
            pltpu.SMEM((6, 4), jnp.int32),
        ),
        [hbm] * 7,
        [
            pltpu.SMEM((1, members), jnp.int32),
            pltpu.SMEM((2, rows), jnp.int32),
            pltpu.SMEM((2, rows), jnp.int32),
            pltpu.SMEM((rows,), jnp.int32),
            pltpu.SMEM((4, rows), jnp.int32),
            pltpu.SMEM(coarse_cols.shape[::-1], jnp.int32),
            pltpu.SemaphoreType.DMA((7,)),
        ],
        8,
        2000,
    )(
        outside(send_rows.reshape(1, members)), outside(p_cols.T), outside(offd_cols.T),
        outside(offd_count), outside(diag_cols.T), outside(coarse_cols.T),
        outside(p_tiles.reshape(2 * rows, T, T)),
    )
    pairs = (
        [(i, i ^ 1) for i in range(members)],
        [(i, (i - 1 if i % 2 == 0 else i + 1) % members) for i in range(members)],
        [(i, (i + half) % members) for i in range(members)],
    )
    got = [None] * 3
    for e in (2, 1, 0):
        got[e] = inside(lax.ppermute(sends[e], "member", pairs[e]))

    far, qs, pt, aq, z = call(
        functools.partial(local_kernel, rows),
        (
            pltpu.VMEM((4, T, T), BF),
            pltpu.VMEM((2, 3, T, 2 * T), BF),
            pltpu.VMEM((2 * rows + 1, T, T), BF),
            pltpu.VMEM((rows, 3, T, T), BF),
            pltpu.VMEM((rows, T, 3 * T), BF),
        ),
        [smem] * 3 + [vmem] * 3,
        [],
        16,
        2000,
    )(slot, live, dcols, inside(pv), inside(offd_tiles), inside(diag_tiles))
    far, qs, pt, aq, z = [inside(x) for x in (far, qs, pt, aq, z)]

    def along_group(x, step):
        return inside(lax.ppermute(x, "group", [(i, (i + step) % groups) for i in range(groups)]))

    rd = pltpu.VMEM((10, T, T), BF)
    six = pltpu.VMEM((6, T, T), BF)
    send1, send4 = call(
        far_kernel,
        (six, six), [smem] + [vmem] * 5, [rd], 8,
    )(chosen, far, qs, *got)
    a4 = along_group(send4, shift)
    a1 = along_group(send1, 1)
    own = call(
        functools.partial(near_kernel, rows),
        pltpu.VMEM((8, T, T), F32), [smem] * 2 + [vmem] * 6,
        [rd, pltpu.VMEM((3, T, 2 * T), BF)], 12, 1000,
    )(chosen, slot, pt, aq, z, *got)
    return pl.pallas_call(
        add_kernel,
        out_shape=jax.ShapeDtypeStruct((1, 8, T, T), F32),
        in_specs=[vmem] * 3,
        out_specs=vmem,
        compiler_params=pltpu.CompilerParams(vmem_limit_bytes=8 << 20),
        name="add",
    )(inside(own), a1, a4)


def solution(mesh):
    return jax.shard_map(
        on_device,
        mesh=mesh,
        in_specs=(
            P(("group", "member"), None, None, None),
            P(("group", "member"), None),
            P(("group", "member"), None, None, None),
            P(("group", "member"), None),
            P(("group", "member")),
            P(("group", "member"), None, None, None),
            P(("group", "member"), None),
            P(("group", "member"), None, None),
            P(),
        ),
        out_specs=P(("group", "member"), None, None, None),
        check_vma=False,
    )
```

```python
import functools

import jax
import jax.numpy as jnp
from jax import lax
from jax.experimental import pallas as pl
from jax.experimental.pallas import tpu as pltpu
from jax.sharding import PartitionSpec as P


T = 128
HDR = 32
BF = jnp.bfloat16
F32 = jnp.float32


def distance(column, group, groups, members):
    return ((column >> (members.bit_length() - 1)) - group) & (groups - 1)


def kind_of(column, group, groups, members):
    rel = distance(column, group, groups, members)
    return jnp.where(rel < 2, rel, jnp.where(rel == groups // 2, 2, 3))


def live_kind_of(column, group, groups, members):
    return jnp.minimum(distance(column, group, groups, members), 2)


def partners_of(member, members):
    odd = lax.rem(member, 2)
    up = lax.rem(member + 1, members)
    down = lax.rem(member + members - 1, members)
    return (
        jnp.where(odd == 1, down, up),
        jnp.where(odd == 1, up, down),
        lax.rem(member + members // 2, members),
    )


def fill_slots(slot_ref, pc_ref, rows, group, groups, members):
    for f in range(rows):
        for q in range(2):
            slot_ref[live_kind_of(pc_ref[q, f], group, groups, members), f] = 2 * f + q


def pick_kernel(
    groups, members, rows,
    send_hbm, pc_hbm, oc_hbm, cnt_hbm, dc_hbm, cc_hbm, p_hbm,
    o0, o1, o2, pv, slot_ref, live_ref, dc_out, pick_ref, place_ref,
    send_ref, pc_ref, oc_ref, cnt_ref, cc_ref, sems,
):
    group = lax.axis_index("group")
    partners = partners_of(lax.axis_index("member"), members)
    copies = [
        pltpu.make_async_copy(src, dst, sems.at[i])
        for i, (src, dst) in enumerate(
            (
                (send_hbm, send_ref),
                (pc_hbm, pc_ref),
                (p_hbm, pv.at[pl.ds(0, 2 * rows)]),
                (oc_hbm, oc_ref),
                (cnt_hbm, cnt_ref),
                (dc_hbm, dc_out),
                (cc_hbm, cc_ref),
            )
        )
    ]
    for copy in copies:
        copy.start()
    pv[2 * rows] = jnp.zeros((T, T), BF)
    for f in range(rows):
        for h in range(3):
            slot_ref[h, f] = 2 * rows
    copies[0].wait()
    copies[1].wait()
    picked = [send_ref[0, partner] for partner in partners]
    for row, out in zip(picked, (o0, o1, o2)):
        for q in range(2):
            kind = live_kind_of(pc_ref[q, row], group, groups, members)
            at = 2 * T + q * (HDR // 2)
            out[at : at + HDR // 2, :] = jnp.full((HDR // 2, T), kind.astype(F32), F32).astype(BF)
    for copy in copies[3:]:
        copy.wait()
    fill_slots(slot_ref, pc_ref, rows, group, groups, members)
    for f in range(rows):
        for k in range(2):
            sender = oc_ref[k, f]
            e = jnp.where(sender == partners[0], 0, jnp.where(sender == partners[1], 1, 2))
            live_ref[k, f] = jnp.where(k < cnt_ref[f], e, 3)
    member = lax.axis_index("member")
    for h in range(3):
        target = ((group + (0, 1, groups // 2)[h]) & (groups - 1)) * members + member
        rank = jnp.int32(0)
        for s in range(cc_ref.shape[0]):
            col = cc_ref[s, target]
            m2 = col & (members - 1)
            e = jnp.where(m2 == partners[0], 0, jnp.where(m2 == partners[1], 1, 2))
            kind = kind_of(col, group, groups, members)
            at = jnp.where(m2 == member, 4, rank)
            pick_ref[2 * h, at] = e
            pick_ref[2 * h + 1, at] = jnp.where(kind == 3, 9, 3 * e + kind)
            if h == 0:
                own = jnp.where(kind == 2, 3, jnp.where(kind == 3, 2, kind))
                place_ref[0, jnp.where(m2 == member, own, 4 + rank)] = s
            rank = rank + jnp.where(m2 == member, 0, 1)
    copies[2].wait()
    for row, out in zip(picked, (o0, o1, o2)):
        out[0:T, :] = pv[2 * row]
        out[T : 2 * T, :] = pv[2 * row + 1]


def left_rows(pt, slot_ref, rows, h):
    return jnp.concatenate([pt[slot_ref[h, f]] for f in range(rows)], axis=1)


def remote_right(rows, aq):
    return jnp.concatenate(
        [jnp.concatenate([aq[f, e] for e in range(3)], axis=1) for f in range(rows)], axis=0
    )


def local_right(rows, z):
    return jnp.concatenate([z[f] for f in range(rows)], axis=0)


def split_into(out, qs):
    for e in range(3):
        block = qs[:, e * T : (e + 1) * T]
        high = block.astype(BF)
        out[e, :, 0:T] = high
        out[e, :, T : 2 * T] = (block - high.astype(F32)).astype(BF)


def local_kernel(rows, slot_ref, live_ref, dc_ref, pv, ov, dv, early_ref, far_ref, q_ref, pt, aq, z):
    zero = jnp.zeros((T, T), BF)
    pt[2 * rows] = zero
    for t in range(2 * rows):
        pt[t] = pv[t].T
    for f in range(rows):
        a = jnp.concatenate([dv[f, k] for k in range(4)], axis=1)
        js = [dc_ref[k, f] for k in range(4)]
        b = jnp.concatenate(
            [jnp.concatenate([pv[slot_ref[h, j]] for h in range(3)], axis=1) for j in js], axis=0
        )
        z[f] = jnp.dot(a, b, preferred_element_type=F32).astype(BF)
        for e in range(3):
            aq[f, e] = lax.select(live_ref[0, f] == e, ov[f, 0], zero) + lax.select(
                live_ref[1, f] == e, ov[f, 1], zero
            )
    lhs = jnp.concatenate([left_rows(pt, slot_ref, rows, h) for h in (1, 2)], axis=0)
    qs = jnp.dot(lhs, remote_right(rows, aq), preferred_element_type=F32)
    gs = jnp.dot(lhs, local_right(rows, z), preferred_element_type=F32).astype(BF)
    for i in range(2):
        split_into(q_ref.at[i], qs[i * T : (i + 1) * T])
    for out, h in ((early_ref, 1), (far_ref, 2)):
        for i, c in enumerate((h, 0)):
            out[i] = gs[(h - 1) * T : h * T, c * T : (c + 1) * T]


def received(pay_refs, rd):
    for e in range(3):
        kinds = [pay_refs[e][2 * T + 16 * q : 2 * T + 16 * q + 16, :].astype(F32) for q in range(2)]
        tiles = [pay_refs[e][q * T : (q + 1) * T, :].reshape(8, 16, T) for q in range(2)]
        for h in range(3):
            masks = [jnp.where(kind == h, 1.0, 0.0).astype(BF)[None] for kind in kinds]
            rd[3 * e + h] = (tiles[0] * masks[0] + tiles[1] * masks[1]).reshape(T, T)
    rd[9] = jnp.zeros((T, T), BF)


def remote_tile(pick_ref, left, rd, h, s):
    tile = rd[pick_ref[2 * h + 1, s]]
    return jnp.dot(
        left[pick_ref[2 * h, s]],
        jnp.concatenate([tile, tile], axis=0),
        preferred_element_type=F32,
    )


def far_kernel(pick_ref, far_ref, q_ref, r0, r1, r2, s1_ref, s4_ref, rd):
    received((r0, r1, r2), rd)
    for h, out in ((2, s4_ref), (1, s1_ref)):
        at = 0 if h == 1 else 2
        for i in range(at):
            out[i] = far_ref[i]
        for s in range(4):
            out[at + s] = remote_tile(pick_ref, q_ref.at[h - 1], rd, h, s).astype(BF)


def near_kernel(rows, pick_ref, slot_ref, pt, aq, z, r0, r1, r2, own_ref, rd, q_ref):
    received((r0, r1, r2), rd)
    lhs = left_rows(pt, slot_ref, rows, 0)
    split_into(q_ref, jnp.dot(lhs, remote_right(rows, aq), preferred_element_type=F32))
    near = jnp.dot(lhs, local_right(rows, z), preferred_element_type=F32)
    own_ref[0] = near[:, 0:T]
    own_ref[1] = near[:, T : 2 * T]
    own_ref[2] = jnp.zeros((T, T), F32)
    own_ref[3] = near[:, 2 * T : 3 * T]
    for s in range(4):
        own_ref[4 + s] = remote_tile(pick_ref, q_ref, rd, 0, s)


def add_kernel(place_ref, own_ref, e_ref, a1_ref, a4_ref, out_hbm, out, sems):
    def write(i, tile):
        out[i] = tile
        copy = pltpu.make_async_copy(out.at[i], out_hbm.at[0, place_ref[0, i]], sems.at[i])
        copy.start()
        return copy

    copies = [
        write(0, own_ref[0] + e_ref[0].astype(F32) + a4_ref[0].astype(F32)),
        write(1, own_ref[1]),
        write(2, own_ref[2] + e_ref[1].astype(F32)),
        write(3, own_ref[3] + a4_ref[1].astype(F32)),
    ]
    for s in range(4):
        tile = own_ref[4 + s] + a1_ref[s].astype(F32) + a4_ref[2 + s].astype(F32)
        copies.append(write(4 + s, tile))
    for copy in copies:
        copy.wait()


def on_device(
    diag_tiles, diag_cols, offd_tiles, offd_cols, offd_count, p_tiles, p_cols, send_rows,
    coarse_cols,
):
    rows = p_tiles.shape[0]
    groups = lax.axis_size("group")
    members = lax.axis_size("member")
    vmem = pl.BlockSpec(memory_space=pltpu.VMEM)
    smem = pl.BlockSpec(memory_space=pltpu.SMEM)
    hbm = pl.BlockSpec(memory_space=pl.ANY)
    half = members // 2
    shift = groups // 2

    def inside(x):
        return pltpu.with_memory_space_constraint(x, pltpu.VMEM)

    def outside(x):
        return pltpu.with_memory_space_constraint(x, pltpu.HBM)

    def call(kernel, out_shape, in_specs, scratch, mib, mflop=10):
        return pl.pallas_call(
            kernel,
            out_shape=out_shape,
            in_specs=in_specs,
            out_specs=jax.tree.map(
                lambda x: pl.BlockSpec(memory_space=x.memory_space),
                out_shape,
                is_leaf=lambda x: not isinstance(x, tuple),
            ),
            scratch_shapes=scratch,
            compiler_params=pltpu.CompilerParams(vmem_limit_bytes=mib << 20),
            cost_estimate=pl.CostEstimate(
                flops=mflop * 10**6, transcendentals=0, bytes_accessed=mflop * 10**4
            ),
        )

    payload = pltpu.VMEM((2 * T + HDR, T), BF)
    *sends, pv, slot, live, dcols, chosen, place = call(
        functools.partial(pick_kernel, groups, members, rows),
        (
            payload, payload, payload, pltpu.VMEM((2 * rows + 1, T, T), BF),
            pltpu.SMEM((3, rows), jnp.int32),
            pltpu.SMEM((2, rows), jnp.int32),
            pltpu.SMEM((4, rows), jnp.int32),
            pltpu.SMEM((6, 5), jnp.int32),
            pltpu.SMEM((1, coarse_cols.shape[1]), jnp.int32),
        ),
        [hbm] * 7,
        [
            pltpu.SMEM((1, members), jnp.int32),
            pltpu.SMEM((2, rows), jnp.int32),
            pltpu.SMEM((2, rows), jnp.int32),
            pltpu.SMEM((rows,), jnp.int32),
            pltpu.SMEM(coarse_cols.shape[::-1], jnp.int32),
            pltpu.SemaphoreType.DMA((7,)),
        ],
        8,
        2000,
    )(
        outside(send_rows.reshape(1, members)), outside(p_cols.T), outside(offd_cols.T),
        outside(offd_count), outside(diag_cols.T), outside(coarse_cols.T),
        outside(p_tiles.reshape(2 * rows, T, T)),
    )
    pairs = (
        [(i, i ^ 1) for i in range(members)],
        [(i, (i - 1 if i % 2 == 0 else i + 1) % members) for i in range(members)],
        [(i, (i + half) % members) for i in range(members)],
    )
    got = [None] * 3
    for e in (2, 1, 0):
        got[e] = inside(lax.ppermute(sends[e], "member", pairs[e]))

    early, far, qs, pt, aq, z = call(
        functools.partial(local_kernel, rows),
        (
            pltpu.VMEM((2, T, T), BF),
            pltpu.VMEM((2, T, T), BF),
            pltpu.VMEM((2, 3, T, 2 * T), BF),
            pltpu.VMEM((2 * rows + 1, T, T), BF),
            pltpu.VMEM((rows, 3, T, T), BF),
            pltpu.VMEM((rows, T, 3 * T), BF),
        ),
        [smem] * 3 + [vmem] * 3,
        [],
        16,
        2000,
    )(slot, live, dcols, inside(pv), inside(offd_tiles), inside(diag_tiles))
    far, qs, pt, aq, z = [inside(x) for x in (far, qs, pt, aq, z)]

    def along_group(x, step):
        return inside(lax.ppermute(x, "group", [(i, (i + step) % groups) for i in range(groups)]))

    sooner = along_group(early, 1)
    rd = pltpu.VMEM((10, T, T), BF)
    four = pltpu.VMEM((4, T, T), BF)
    six = pltpu.VMEM((6, T, T), BF)
    send1, send4 = call(
        far_kernel,
        (four, six), [smem] + [vmem] * 5, [rd], 8,
    )(chosen, far, qs, *got)
    a4 = along_group(send4, shift)
    a1 = along_group(send1, 1)
    own = call(
        functools.partial(near_kernel, rows),
        pltpu.VMEM((8, T, T), F32), [smem] * 2 + [vmem] * 6,
        [rd, pltpu.VMEM((3, T, 2 * T), BF)], 12, 1000,
    )(chosen, slot, pt, aq, z, *got)
    return pl.pallas_call(
        add_kernel,
        out_shape=jax.ShapeDtypeStruct((1, 8, T, T), F32),
        in_specs=[smem] + [vmem] * 4,
        out_specs=hbm,
        scratch_shapes=[pltpu.VMEM((8, T, T), F32), pltpu.SemaphoreType.DMA((8,))],
        compiler_params=pltpu.CompilerParams(vmem_limit_bytes=8 << 20),
        name="add",
    )(place, inside(own), sooner, a1, a4)


def solution(mesh):
    return jax.shard_map(
        on_device,
        mesh=mesh,
        in_specs=(
            P(("group", "member"), None, None, None),
            P(("group", "member"), None),
            P(("group", "member"), None, None, None),
            P(("group", "member"), None),
            P(("group", "member")),
            P(("group", "member"), None, None, None),
            P(("group", "member"), None),
            P(("group", "member"), None, None),
            P(),
        ),
        out_specs=P(("group", "member"), None, None, None),
        check_vma=False,
    )
```
